32 devices in a mesh: group: 4 (over y, x), dom: 8 (over z, core).
Axes of the slice: x: 2, y: 2, z: 4, core: 2. Of those that a mesh axis runs over, the one named last changes fastest.
Arguments:
- features: bfloat16 [2, 8192, 1024], P(None, ('group', 'dom')), may hold values from -6 to 6
- adjacency: bfloat16 [8192, 256], P(('group', 'dom')), may hold values from -0.375 to 0.375
- tile_mask: int32 [64, 2], P(('group', 'dom')), may hold values 0 or 1
- boundary_adj: bfloat16 [8192, 1024], P(('group', 'dom')), may hold values from -0.1875 to 0.1875
- boundary_blocks: int32 [4, 8, 4, 2], P('group'), may hold values from -1 to 1
- hub_adj: bfloat16 [32, 8192], P(None, ('group', 'dom')), may hold values from -0.125 to 0.125
- hub_offsets: int32 [4, 32], P('group', 'dom'), may hold values from 0 to 63
- weight: bfloat16 [1024, 1024], replicated, may hold values from -0.1875 to 0.1875
- cotangent: bfloat16 [2, 8192, 1024], P(None, ('group', 'dom')), may hold values from -6 to 6
Outputs:
- activations: bfloat16 [2, 8192, 1024], P(None, ('group', 'dom'))
- input_grad: bfloat16 [2, 8192, 1024], P(None, ('group', 'dom'))
- carried_grad: bfloat16 [8192, 1024], P(('group', 'dom'))
- weight_grad: float32 [1024, 1024], P(('group', 'dom'))
The draws below stay inside these ranges and needn't reach their ends.
Inputs may be any that keep to these rules, and one draw needn't show every extreme that they name: `boundary_blocks`: entry [g, d, o, j] names the block that cluster (g, d) requests in slot j from the cluster at dom index d + s_o (s_o as in the reference program); -1 marks an unused slot; a slot whose source lies outside the group receives zeros. `hub_offsets`: gives the row of hub h's mirror in cluster (g, h // 4) as stated in the reference program. `tile_mask`: 1 where a tile of local edges is present.
All inputs are finite; a program needn't handle non-finite values. No bound on the sum of `tile_mask` on one device may be relied on, other than what follows from the above.
Results may differ from the reference program's by a relative error of at most 0.0067.
Values may be sent and summed in bfloat16 or wider, within the bound.
A program may use at most 64 MiB of HBM per device.

```python
import jax
import jax.numpy as jnp
from jax import lax

D = 1024
NODES = 256
BLK = 128
CAPB = 2
HUB_DEV = 4
ITERS = 2
NB = 2
OFFS = 4
SLOTS = 8
GROUPS = 4
DOMS = 8
ALLNODES = 8192
HUBS = 32
ALLTILES = 64


def touch_ends(drawn, rng, least, top_value):
    longest = drawn.shape.index(max(drawn.shape))
    spots = []
    for shift in (0, 1):
        where = [jax.random.randint(jax.random.fold_in(rng, axis), (), 0, length) for axis, length in enumerate(drawn.shape)]
        where[longest] = (where[longest] + shift) % drawn.shape[longest]
        spots.append(tuple(where))
    return drawn.at[spots[0]].set(least).at[spots[1]].set(top_value)


def strengthened(drawn, key, source, target, blocks, factor):
    owner, partner = [(jnp.arange(drawn.shape[dim]) // (drawn.shape[dim] // blocks)).reshape([-1 if axis == dim else 1 for axis in range(drawn.ndim)]) for dim in (source, target)]
    chosen = jax.random.permutation(key, blocks)[partner]
    strong = (owner == chosen) | (owner == (partner + blocks // 2) % blocks)
    return jnp.where(strong, factor * drawn, drawn)


def block_levels(key, dims, cuts, low, largest):
    loudness = 1.0
    for dim, blocks in cuts:
        steps = jax.random.uniform(jax.random.fold_in(jax.random.fold_in(key, 6), dim), (blocks,), jnp.float32, low / len(cuts), largest / len(cuts))
        loudness = loudness * jnp.repeat(jnp.exp(steps), dims[dim] // blocks).reshape((-1,) + (1,) * (len(dims) - 1 - dim))
    return loudness


def bell_draw(rng, shape, width, limit, split=(), kind=jnp.bfloat16):
    factor_of = block_levels(rng, shape, split, -0.22, 0.18) if split else 1.0
    entries = jax.random.normal(rng, shape, jnp.float32) * width * factor_of
    return jnp.minimum(jnp.maximum(entries, -limit), limit).astype(kind)


def bell_draw_with(own_key, dims, scale, bound, cuts, heavy, held_as=jnp.bfloat16):
    drawn = scale * jax.random.normal(own_key, dims, jnp.float32)
    if cuts:
        drawn = drawn * block_levels(own_key, dims, cuts, -0.22, 0.18)
    return jnp.clip(strengthened(drawn, jax.random.fold_in(own_key, 3), *heavy), -bound, bound).astype(held_as)


def setup_inputs(seed: int = 0) -> dict:
    seeds = jax.random.split(jax.random.key(seed), 10)
    return {
        "features": bell_draw(seeds[0], (ITERS, ALLNODES, D), 1.0, 6.0, ((1, 32),)),
        "adjacency": bell_draw(seeds[1], (ALLNODES, NODES), NODES ** -0.5, 0.375, ((0, 32),)),
        "tile_mask": touch_ends((jax.random.randint(seeds[2], (ALLTILES, NB), 0, 4) < 3).astype(jnp.int32), jax.random.fold_in(seeds[2], 1), 0, 1),
        "boundary_adj": bell_draw(seeds[3], (ALLNODES, SLOTS * BLK), (SLOTS * BLK) ** -0.5, 0.1875, ((0, 32),)),
        "boundary_blocks": touch_ends(jax.random.randint(seeds[4], (GROUPS, DOMS, OFFS, CAPB), -1, NB), jax.random.fold_in(seeds[4], 1), -1, NB - 1).astype(jnp.int32),
        "hub_adj": bell_draw_with(seeds[5], (HUBS, ALLNODES), ALLNODES ** -0.5, 0.125, ((1, 32),), (1, 0, 32, 2.75)),
        "hub_offsets": touch_ends(jax.random.randint(seeds[6], (GROUPS, HUBS), 0, NODES // HUB_DEV), jax.random.fold_in(seeds[6], 1), 0, (NODES // HUB_DEV) - 1).astype(jnp.int32),
        "weight": bell_draw(seeds[7], (D, D), D ** -0.5, 0.1875),
        "cotangent": bell_draw_with(seeds[8], (ITERS, ALLNODES, D), 1.0, 6.0, ((1, 32),), (1, 2, 32, 2.75)),
    }


def offset_of(order):
    return (order // 2 + 1) * (1 - 2 * (order % 2))


def reference(features, adjacency, tile_mask, boundary_adj, boundary_blocks, hub_adj, hub_offsets, weight, cotangent):
    devs = GROUPS * DOMS
    spread = jnp.repeat(jnp.repeat(tile_mask.reshape(devs, NB, NB), BLK, axis=1), BLK, axis=2).astype(jnp.bfloat16)
    local_adj = adjacency.reshape(devs, NODES, NODES) * spread
    bound_adj = boundary_adj.reshape(devs, NODES, SLOTS * BLK)
    hub_cols = jnp.transpose(hub_adj.reshape(HUBS, devs, NODES), (1, 0, 2))
    stride = NODES // HUB_DEV
    hub_rows = ((jnp.arange(HUBS, dtype=jnp.int32) % HUB_DEV) * stride)[None, :] + hub_offsets
    hub_rows = hub_rows.astype(jnp.int32).reshape(devs, HUB_DEV)
    shifts = jnp.array([offset_of(o) for o in range(OFFS)], dtype=jnp.int32)
    source = jnp.arange(DOMS, dtype=jnp.int32)[:, None] + shifts[None, :]
    inside = (source >= 0) & (source < DOMS)
    source = jnp.clip(source, 0, DOMS - 1).astype(jnp.int32)
    live = (boundary_blocks >= 0) & inside[None, :, :, None]
    block = jnp.clip(boundary_blocks, 0, NB - 1).astype(jnp.int32)
    groups = jnp.arange(GROUPS, dtype=jnp.int32)[:, None]
    first = features[0].reshape(GROUPS, DOMS, NB, BLK, D)
    pieces = []
    for o in range(OFFS):
        for j in range(CAPB):
            got = first[groups, source[None, :, o], block[:, :, o, j]]
            pieces.append(jnp.where(live[:, :, o, j][:, :, None, None], got, jnp.zeros_like(got)))
    received = jnp.stack(pieces, axis=2).reshape(devs, SLOTS * BLK, D)
    scale = (ITERS * NODES * devs) ** -0.5
    acts, grads = [], []
    weight_total = jnp.zeros((D, D), jnp.float32)
    carried = jnp.zeros((GROUPS, DOMS, NB, BLK, D), jnp.float32)
    for step in range(ITERS):
        feats = features[step].reshape(devs, NODES, D)
        hub_sum = jnp.dot(hub_adj, features[step], preferred_element_type=jnp.float32)
        hub_blocks = jnp.broadcast_to(hub_sum.reshape(1, DOMS, HUB_DEV, D), (GROUPS, DOMS, HUB_DEV, D)).reshape(devs, HUB_DEV, D)
        cot = cotangent[step].reshape(devs, NODES, D)

        def forward(items):
            adj, bnd, feat, recv, rows, hubs, grad_out = items
            total = jnp.dot(adj, feat, preferred_element_type=jnp.float32) + jnp.dot(bnd, recv, preferred_element_type=jnp.float32)
            total = total.at[rows].add(hubs)
            agg = total.astype(jnp.bfloat16)
            pre = jnp.dot(agg, weight.T, preferred_element_type=jnp.float32)
            act = jax.nn.silu(pre).astype(jnp.bfloat16)
            sig = jax.nn.sigmoid(pre)
            gpre = (grad_out.astype(jnp.float32) * sig * (1.0 + pre * (1.0 - sig))).astype(jnp.bfloat16)
            dagg = jnp.dot(gpre, weight, preferred_element_type=jnp.float32).astype(jnp.bfloat16)
            local = jnp.dot(adj.T, dagg, preferred_element_type=jnp.float32)
            bgrad = jnp.dot(bnd.T, dagg, preferred_element_type=jnp.float32).astype(jnp.bfloat16)
            mirror = dagg[rows]
            return agg, act, gpre, local, bgrad, mirror

        agg, act, gpre, local, bgrad, mirror = lax.map(forward, (local_adj, bound_adj, feats, received, hub_rows, hub_blocks, cot))
        hub_grad = jnp.sum(mirror.reshape(GROUPS, HUBS, D).astype(jnp.float32), axis=0)

        def hub_back(cols):
            return jnp.dot(cols.astype(jnp.float32).T, hub_grad, precision=lax.Precision.HIGHEST)

        hub_term = lax.map(hub_back, hub_cols)
        back = jnp.zeros((GROUPS, DOMS, NB, BLK, D), jnp.float32)
        slots = bgrad.reshape(GROUPS, DOMS, OFFS, CAPB, BLK, D)
        for o in range(OFFS):
            for j in range(CAPB):
                vals = jnp.where(live[:, :, o, j][:, :, None, None], slots[:, :, o, j].astype(jnp.float32), jnp.zeros((GROUPS, DOMS, BLK, D), jnp.float32))
                back = back.at[groups, source[None, :, o], block[:, :, o, j]].add(vals)
        grads.append((local + hub_term + carried.reshape(devs, NODES, D)).astype(jnp.bfloat16).reshape(ALLNODES, D))
        acts.append(act.reshape(ALLNODES, D))
        carried = back
        weight_total = weight_total + jnp.dot(gpre.reshape(ALLNODES, D).T, agg.reshape(ALLNODES, D), preferred_element_type=jnp.float32)
    return (jnp.stack(acts), jnp.stack(grads), carried.reshape(ALLNODES, D).astype(jnp.bfloat16), weight_total * scale)
```

```python
import functools

import jax
import jax.numpy as jnp
from jax import lax
from jax.experimental import pallas as pl
from jax.experimental.pallas import tpu as pltpu
from jax.sharding import PartitionSpec as P

BLK = 128
TILE = 256
HALVES = 2
MESH = pl.DeviceIdType.MESH
F32 = jnp.float32
BF16 = jnp.bfloat16


def offset_of(order):
    return (order // 2 + 1) * (1 - 2 * (order % 2))


def mm(left, right):
    return jnp.dot(left, right, preferred_element_type=F32)


def mm_nt(left, right):
    return lax.dot_general(left, right, (((1,), (1,)), ((), ())), preferred_element_type=F32)


def mm_tn(left, right):
    return lax.dot_general(left, right, (((0,), (0,)), ((), ())), preferred_element_type=F32)


def kernel(
    cfg,
    feats, adj, mask, badj, bblocks, hub, offs, weight_hbm, cot_hbm,
    act, igrad, carried, wout,
    rx, rsel, hp, hrx, hs, hgx, hubsum, mr, mgx, ms, mdx,
    la, lat, bt, loc, base, aggs, gps, dg, gs, gx, back,
    weight, cot, ws, w1, w2s, w2r, w3s, w3r,
    load_sem, f_send, f_recv, h_send, h_recv, hg_send, hg_recv,
    m_send, m_recv, md_send, md_recv, g_send, g_recv,
    w1_send, w1_recv, w2_send, w2_recv, w3_send, w3_recv,
):
    iters, nodes, width, doms, groups, hubdev, orders, cap, scatter, scale = cfg
    half = width // HALVES
    chips = doms // 2
    tiles = width // TILE
    d = lax.axis_index("dom")
    g = lax.axis_index("group")
    c = lax.rem(d, 2)
    z = lax.div(d, 2)
    partner = d + 1 - 2 * c
    hubs = doms * hubdev
    rows8 = iters * hubdev

    load_w = pltpu.make_async_copy(weight_hbm, weight, load_sem.at[0])
    load_c = pltpu.make_async_copy(cot_hbm, cot, load_sem.at[1])
    load_w.start()
    load_c.start()

    barrier = pltpu.get_barrier_semaphore()

    def greet_dom(k, _):
        pl.semaphore_signal(barrier, inc=1, device_id={"dom": lax.rem(d + k, doms)}, device_id_type=MESH)
        return 0

    def greet_group(k, _):
        pl.semaphore_signal(barrier, inc=1, device_id={"group": lax.rem(g + k, groups)}, device_id_type=MESH)
        return 0

    lax.fori_loop(1, doms, greet_dom, 0)
    lax.fori_loop(1, groups, greet_group, 0)

    r = lax.broadcasted_iota(jnp.int32, (doms * rows8, hubs), 0)
    q = lax.broadcasted_iota(jnp.int32, (doms * rows8, hubs), 1)
    spread = []
    for t in range(iters):
        hit = (r // rows8 == q // hubdev) & (r % rows8 == t * hubdev + q % hubdev)
        spread.append(jnp.where(hit, 1.0, 0.0).astype(BF16))
    hub_rows = [mm(spread[t], hub[...]).astype(BF16) for t in range(iters)]

    @pl.loop(0, tiles)
    def _(i):
        cols = pl.ds(pl.multiple_of(i * TILE, TILE), TILE)
        total = mm(hub_rows[0], feats[0, :, cols])
        for t in range(1, iters):
            total = total + mm(hub_rows[t], feats[t, :, cols])
        hp[:, :, cols] = total.reshape(doms, rows8, TILE)

    pl.semaphore_wait(barrier, doms + groups - 2)

    def f_copy(kind, b, src, dst_slot, device):
        return pltpu.make_async_remote_copy(
            src_ref=src.at[pl.ds(b * BLK, BLK), :],
            dst_ref=rx.at[dst_slot, pl.ds(b * BLK, BLK), :],
            send_sem=f_send.at[kind, b],
            recv_sem=f_recv.at[dst_slot, b],
            device_id={"dom": device},
            device_id_type=MESH,
        )

    up = d + 2 < doms
    down = d >= 2
    relays = jnp.where(c == 1, d >= 2, d + 2 < doms)
    relayed = jnp.where(c == 1, partner + 2 < doms, partner >= 2)
    own = feats.at[0]
    nb = nodes // BLK
    up_to = jnp.minimum(d + 2, doms - 1)
    down_to = jnp.maximum(d - 2, 0)
    for b in range(nb):
        @pl.when(up)
        def _():
            f_copy(0, b, own, 3, up_to).start()

        @pl.when(down)
        def _():
            f_copy(1, b, own, 2, down_to).start()

    def h_copy(k):
        e = lax.rem(d + k, doms)
        return pltpu.make_async_remote_copy(
            src_ref=hp.at[e], dst_ref=hrx.at[k], send_sem=h_send.at[k], recv_sem=h_recv.at[k],
            device_id={"dom": e}, device_id_type=MESH)

    def each(count, body):
        def step(k, _):
            body(k)
            return 0
        lax.fori_loop(1, count, step, 0)

    each(doms, lambda k: h_copy(k).start())
    for b in range(nb):
        f_copy(2, b, own, 1 - c, partner).start()

    for i in range(nb):
        for j in range(nb):
            m = mask[i, j].astype(F32)
            la[i * BLK:(i + 1) * BLK, j * BLK:(j + 1) * BLK] = (
                adj[i * BLK:(i + 1) * BLK, j * BLK:(j + 1) * BLK].astype(F32) * m
            ).astype(BF16)
    lat[...] = la[...].T
    for o in range(orders):
        bt[o * cap * BLK:(o + 1) * cap * BLK, :] = badj[:, o * cap * BLK:(o + 1) * cap * BLK].T

    @pl.loop(0, tiles)
    def _(i):
        cols = pl.ds(pl.multiple_of(i * TILE, TILE), TILE)
        for t in range(iters):
            loc[t, :, cols] = mm(la[...], feats[t, :, cols])

    def add_h(k, total):
        h_copy(k).wait_recv()
        return total + hrx[k]

    hs[...] = lax.fori_loop(1, doms, add_h, hp[d])

    def hg_copy(k):
        e = lax.rem(g + k, groups)
        return pltpu.make_async_remote_copy(
            src_ref=hs, dst_ref=hgx.at[k], send_sem=hg_send.at[k], recv_sem=hg_recv.at[k],
            device_id={"group": e}, device_id_type=MESH)

    each(groups, lambda k: hg_copy(k).start())

    for b in range(nb):
        @pl.when(relays)
        def _():
            f_copy(0, b, own, 2 + c, partner).wait_recv()
            f_copy(3, b, rx.at[2 + c], c, partner).start()

    def pick(o):
        for j in range(cap):
            want = bblocks[0, d, o, j]
            m0 = (want == 0).astype(F32)
            m1 = (want == 1).astype(F32)
            start = (o * cap + j) * BLK
            rsel[start:start + BLK, :] = (
                rx[o, 0:BLK, :].astype(F32) * m0 + rx[o, BLK:2 * BLK, :].astype(F32) * m1
            ).astype(BF16)

    def wait_slot(o):
        for b in range(nb):
            f_copy(0, b, own, o, partner).wait_recv()

    for o in (0, 1):
        first = jnp.where(c == o, True, relayed)
        @pl.when(first)
        def _():
            wait_slot(o)
            pick(o)

        @pl.when(jnp.logical_not(first))
        def _():
            rsel[o * cap * BLK:(o + 1) * cap * BLK, :] = jnp.zeros((cap * BLK, width), BF16)

    for o, there in ((2, up), (3, down)):
        @pl.when(there)
        def _():
            @pl.when(c != o - 2)
            def _():
                wait_slot(o)
            pick(o)

        @pl.when(jnp.logical_not(there))
        def _():
            rsel[o * cap * BLK:(o + 1) * cap * BLK, :] = jnp.zeros((cap * BLK, width), BF16)

    @pl.loop(0, tiles)
    def _(i):
        cols = pl.ds(pl.multiple_of(i * TILE, TILE), TILE)
        base[:, cols] = mm(badj[...], rsel[:, cols])

    def add_hg(k, total):
        hg_copy(k).wait_recv()
        return total + hgx[k]

    hubsum[...] = lax.fori_loop(1, groups, add_hg, hs[...])
    load_w.wait()
    load_c.wait()

    stride = nodes // hubdev
    spot = lax.broadcasted_iota(jnp.int32, (stride, TILE), 0)

    def g_copy(t, o):
        e = jnp.clip(d + offset_of(o), 0, doms - 1)
        return pltpu.make_async_remote_copy(
            src_ref=gs.at[t, o], dst_ref=gx.at[t, o], send_sem=g_send.at[t, o], recv_sem=g_recv.at[t, o],
            device_id={"dom": e}, device_id_type=MESH)

    def reaches(o, sign):
        to = d + sign * offset_of(o)
        return (to >= 0) & (to < doms)

    for t in range(iters):
        lo = t * nodes

        @pl.loop(0, tiles)
        def _(i):
            cols = pl.ds(pl.multiple_of(i * TILE, TILE), TILE)
            for k in range(hubdev):
                part = slice(k * stride, (k + 1) * stride)
                total = loc[t, part, cols] + base[part, cols]
                add = jnp.where(spot == offs[0, k], hubsum[t * hubdev + k:t * hubdev + k + 1, cols], 0.0)
                aggs[lo + k * stride:lo + (k + 1) * stride, cols] = (total + add).astype(BF16)

        @pl.loop(0, tiles)
        def _(i):
            cols = pl.ds(pl.multiple_of(i * TILE, TILE), TILE)
            pre = mm_nt(aggs[lo:lo + nodes, :], weight[cols, :])
            sig = 1.0 / (1.0 + jnp.exp(-pre))
            act[t, :, cols] = (pre * sig).astype(BF16)
            gps[lo:lo + nodes, cols] = (
                cot[t, :, cols].astype(F32) * sig * (1.0 + pre * (1.0 - sig))).astype(BF16)

        @pl.loop(0, tiles)
        def _(i):
            cols = pl.ds(pl.multiple_of(i * TILE, TILE), TILE)
            dagg = mm(gps[lo:lo + nodes, :], weight[:, cols]).astype(BF16)
            dg[t, :, cols] = dagg
            for k in range(hubdev):
                rows = dagg[k * stride:(k + 1) * stride, :].astype(F32)
                hit = jnp.where(spot == offs[0, k], rows, 0.0)
                mr[t * hubdev + k:t * hubdev + k + 1, cols] = jnp.sum(hit, axis=0, keepdims=True)

        for o in (2, 3, 0, 1):
            @pl.loop(0, tiles)
            def _(i):
                cols = pl.ds(pl.multiple_of(i * TILE, TILE), TILE)
                gs[t, o, :, cols] = mm(bt[o * cap * BLK:(o + 1) * cap * BLK, :], dg[t, :, cols]).astype(BF16)

            @pl.when(reaches(o, 1))
            def _():
                g_copy(t, o).start()

    def m_copy(k):
        e = lax.rem(g + k, groups)
        return pltpu.make_async_remote_copy(
            src_ref=mr, dst_ref=mgx.at[k], send_sem=m_send.at[k], recv_sem=m_recv.at[k],
            device_id={"group": e}, device_id_type=MESH)

    each(groups, lambda k: m_copy(k).start())

    devices = doms * groups
    if scatter:
        rows = width // devices
        per = BLK // rows

        def w1_copy(h):
            return pltpu.make_async_remote_copy(
                src_ref=ws.at[h, 1 - c], dst_ref=w1.at[h], send_sem=w1_send.at[h], recv_sem=w1_recv.at[h],
                device_id={"dom": partner}, device_id_type=MESH)

        for h in range(HALVES):
            @pl.loop(0, width // BLK)
            def _(i):
                lhs = gps[:, pl.ds(pl.multiple_of(i * BLK, BLK), BLK)]
                res = mm_tn(lhs, aggs[:, h * half:(h + 1) * half]).astype(BF16)
                for p in range(per):
                    f = i * per + p
                    ws[h, p % 2, f // 2] = res[p * rows:(p + 1) * rows, :]
            w1_copy(h).start()
    else:
        @pl.loop(0, width // BLK)
        def _(i):
            at = pl.ds(pl.multiple_of(i * BLK, BLK), BLK)
            wout[at, :] = mm_tn(gps[:, at], aggs[...])

    @pl.loop(0, tiles)
    def _(i):
        cols = pl.ds(pl.multiple_of(i * TILE, TILE), TILE)
        for t in range(iters):
            loc[t, :, cols] = mm(lat[...], dg[t, :, cols])

    def add_m(k, total):
        m_copy(k).wait_recv()
        return total + mgx[k]

    ms[...] = lax.fori_loop(1, groups, add_m, mr[...])

    def md_copy(k):
        e = lax.rem(d + k, doms)
        return pltpu.make_async_remote_copy(
            src_ref=ms, dst_ref=mdx.at[d], send_sem=md_send.at[k], recv_sem=md_recv.at[k],
            device_id={"dom": e}, device_id_type=MESH)

    each(doms, lambda k: md_copy(k).start())

    if scatter:
        def w2_copy(h, k):
            e = lax.rem(g + k, groups)
            return pltpu.make_async_remote_copy(
                src_ref=w2s.at[h, pl.ds(e * chips, chips)], dst_ref=w2r.at[h, k],
                send_sem=w2_send.at[h, k], recv_sem=w2_recv.at[h, k],
                device_id={"group": e}, device_id_type=MESH)

        def w3_copy(h, k):
            e = lax.rem(z + k, chips)
            return pltpu.make_async_remote_copy(
                src_ref=w3s.at[h, e], dst_ref=w3r.at[h, k],
                send_sem=w3_send.at[h, k], recv_sem=w3_recv.at[h, k],
                device_id={"dom": e * 2 + c}, device_id_type=MESH)

        for h in range(HALVES):
            w1_copy(h).wait_recv()

            @pl.loop(0, groups * chips)
            def _(i):
                w2s[h, i] = (ws[h, c, i].astype(F32) + w1[h, i].astype(F32)).astype(BF16)
            for k in range(1, groups):
                w2_copy(h, k).start()

        for h in range(HALVES):
            for k in range(1, groups):
                w2_copy(h, k).wait_recv()

            @pl.loop(0, chips)
            def _(i):
                total = w2s[h, g * chips + i].astype(F32)
                for k in range(1, groups):
                    total = total + w2r[h, k, i].astype(F32)
                w3s[h, i] = total.astype(BF16)
            each(chips, lambda k: w3_copy(h, k).start())

    mdx[d] = ms[...]
    each(doms, lambda k: pltpu.make_async_remote_copy(
        src_ref=ms, dst_ref=mdx.at[lax.rem(d + doms - k, doms)], send_sem=md_send.at[k], recv_sem=md_recv.at[k],
        device_id={"dom": partner}, device_id_type=MESH).wait_recv())
    hub_cols = [mm_tn(hub[...], spread[t].T).astype(BF16) if False else
                lax.dot_general(hub[...], spread[t], (((0,), (1,)), ((), ())), preferred_element_type=F32).astype(BF16)
                for t in range(iters)]

    def add_hubs(i):
        cols = pl.ds(pl.multiple_of(i * TILE, TILE), TILE)
        piece = mdx[:, :, cols].reshape(doms * rows8, TILE)
        upper = piece.astype(BF16)
        lower = (piece - upper.astype(F32)).astype(BF16)
        for t in range(iters):
            total = loc[t, :, cols] + mm(hub_cols[t], upper) + mm(hub_cols[t], lower)
            if t == 0:
                igrad[0, :, cols] = total.astype(BF16)
            else:
                loc[t, :, cols] = total

    pl.loop(0, tiles)(add_hubs)

    for t in range(iters):
        if t + 1 < iters:
            acc = loc.at[t + 1]
        else:
            acc = back
            back[...] = jnp.zeros((nodes, width), F32)
        for o in (0, 1, 2, 3):
            @pl.when(reaches(o, -1))
            def _():
                g_copy(t, o).wait_recv()
                asker = jnp.clip(d - offset_of(o), 0, doms - 1)
                for j in range(cap):
                    want = bblocks[0, asker, o, j]
                    val = gx[t, o, j * BLK:(j + 1) * BLK, :].astype(F32)
                    for b in range(nb):
                        acc[b * BLK:(b + 1) * BLK, :] += val * (want == b).astype(F32)
        if t + 1 < iters:
            igrad[t + 1] = acc[...].astype(BF16)
        else:
            carried[...] = acc[...].astype(BF16)

    if scatter:
        for h in range(HALVES):
            each(chips, lambda k: w3_copy(h, k).wait_recv())
            total = w3s[h, z].astype(F32)
            for k in range(1, chips):
                total = total + w3r[h, k].astype(F32)
            wout[:, h * half:(h + 1) * half] = total * scale

    for b in range(nb):
        @pl.when(up)
        def _():
            f_copy(0, b, own, 3, up_to).wait_send()

        @pl.when(down)
        def _():
            f_copy(1, b, own, 2, down_to).wait_send()

        f_copy(2, b, own, 1 - c, partner).wait_send()

        @pl.when(relays)
        def _():
            f_copy(3, b, rx.at[2 + c], c, partner).wait_send()
    each(doms, lambda k: h_copy(k).wait_send())
    each(groups, lambda k: hg_copy(k).wait_send())
    each(groups, lambda k: m_copy(k).wait_send())
    each(doms, lambda k: md_copy(k).wait_send())
    for t in range(iters):
        for o in range(orders):
            @pl.when(reaches(o, 1))
            def _():
                g_copy(t, o).wait_send()
    if scatter:
        for h in range(HALVES):
            w1_copy(h).wait_send()
            for k in range(1, groups):
                w2_copy(h, k).wait_send()
            each(chips, lambda k: w3_copy(h, k).wait_send())


def per_device(features, adjacency, tile_mask, boundary_adj, boundary_blocks, hub_adj, hub_offsets, weight, cotangent):
    iters, nodes, width = features.shape
    orders, cap = boundary_blocks.shape[2:]
    doms = lax.axis_size("dom")
    groups = lax.axis_size("group")
    devices = doms * groups
    hubdev = hub_offsets.shape[1]
    chips = doms // 2
    rows = width // devices
    rows8 = iters * hubdev
    half = width // HALVES
    scatter = rows % 16 == 0 and BLK % (2 * rows) == 0
    scale = (iters * nodes * devices) ** (-0.5)
    cfg = (iters, nodes, width, doms, groups, hubdev, orders, cap, scatter, scale)
    dma = pltpu.SemaphoreType.DMA
    vmem = pltpu.VMEM
    wshape = (rows, half) if scatter else (16, 128)
    wide = groups * chips if scatter else 1
    deep = chips if scatter else 1
    scratch = [
        vmem((orders, nodes, width), BF16),
        vmem((orders * cap * BLK, width), BF16),
        vmem((doms, rows8, width), F32),
        vmem((doms, rows8, width), F32),
        vmem((rows8, width), F32),
        vmem((groups, rows8, width), F32),
        vmem((rows8, width), F32),
        vmem((rows8, width), F32),
        vmem((groups, rows8, width), F32),
        vmem((rows8, width), F32),
        vmem((doms, rows8, width), F32),
        vmem((nodes, nodes), BF16),
        vmem((nodes, nodes), BF16),
        vmem((orders * cap * BLK, nodes), BF16),
        vmem((iters, nodes, width), F32),
        vmem((nodes, width), F32),
        vmem((iters * nodes, width), BF16),
        vmem((iters * nodes, width), BF16),
        vmem((iters, nodes, width), BF16),
        vmem((iters, orders, cap * BLK, width), BF16),
        vmem((iters, orders, cap * BLK, width), BF16),
        vmem((nodes, width), F32),
        vmem(weight.shape, BF16),
        vmem(cotangent.shape, BF16),
        vmem((HALVES, 2, wide) + wshape, BF16),
        vmem((HALVES, wide) + wshape, BF16),
        vmem((HALVES, wide) + wshape, BF16),
        vmem((HALVES, groups, deep) + wshape, BF16),
        vmem((HALVES, deep) + wshape, BF16),
        vmem((HALVES, deep) + wshape, BF16),
        dma((2,)), dma((4, nodes // BLK)), dma((4, nodes // BLK)),
        dma((doms,)), dma((doms,)), dma((groups,)), dma((groups,)),
        dma((groups,)), dma((groups,)), dma((doms,)), dma((doms,)),
        dma((iters, orders)), dma((iters, orders)),
        dma((HALVES,)), dma((HALVES,)), dma((HALVES, groups)), dma((HALVES, groups)),
        dma((HALVES, chips)), dma((HALVES, chips)),
    ]
    in_vmem = pl.BlockSpec(memory_space=pltpu.VMEM)
    in_smem = pl.BlockSpec(memory_space=pltpu.SMEM)
    anywhere = pl.BlockSpec(memory_space=pl.ANY)
    act, igrad, carried, wgrad = pl.pallas_call(
        functools.partial(kernel, cfg),
        out_shape=(
            jax.ShapeDtypeStruct(features.shape, BF16),
            jax.ShapeDtypeStruct(features.shape, BF16),
            jax.ShapeDtypeStruct((nodes, width), BF16),
            jax.ShapeDtypeStruct((rows if scatter else width, width), F32),
        ),
        in_specs=[in_vmem, in_vmem, in_smem, in_vmem, in_smem, in_vmem, in_smem, anywhere, anywhere],
        out_specs=(in_vmem,) * 4,
        scratch_shapes=scratch,
        compiler_params=pltpu.CompilerParams(
            collective_id=0, has_side_effects=True, vmem_limit_bytes=60 * 1024 * 1024),
        cost_estimate=pl.CostEstimate(flops=6 * 10**9, bytes_accessed=10**7, transcendentals=10**6),
    )(features, adjacency, tile_mask, boundary_adj, boundary_blocks, hub_adj, hub_offsets, weight, cotangent)
    if not scatter:
        wgrad = scale * lax.psum_scatter(wgrad, ("group", "dom"), scatter_dimension=0, tiled=True)
    return act, igrad, carried, wgrad


def solution(mesh):
    return jax.shard_map(
        per_device,
        mesh=mesh,
        in_specs=(
            P(None, ("group", "dom"), None),
            P(("group", "dom"), None),
            P(("group", "dom"), None),
            P(("group", "dom"), None),
            P("group", None, None, None),
            P(None, ("group", "dom")),
            P("group", "dom"),
            P(),
            P(None, ("group", "dom"), None),
        ),
        out_specs=(
            P(None, ("group", "dom"), None),
            P(None, ("group", "dom"), None),
            P(("group", "dom"), None),
            P(("group", "dom"), None),
        ),
        check_vma=False,
    )
```

```python
import functools

import jax
import jax.numpy as jnp
from jax import lax
from jax.experimental import pallas as pl
from jax.experimental.pallas import tpu as pltpu
from jax.sharding import PartitionSpec as P

BLK = 128
TILE = 256
HALVES = 2
MESH = pl.DeviceIdType.MESH
F32 = jnp.float32
BF16 = jnp.bfloat16


def offset_of(order):
    return (order // 2 + 1) * (1 - 2 * (order % 2))


def mm(left, right):
    return jnp.dot(left, right, preferred_element_type=F32)


def mm_nt(left, right):
    return lax.dot_general(left, right, (((1,), (1,)), ((), ())), preferred_element_type=F32)


def mm_tn(left, right):
    return lax.dot_general(left, right, (((0,), (0,)), ((), ())), preferred_element_type=F32)


def kernel(
    cfg,
    feats, adj, mask, badj, bblocks, hub, offs, weight_hbm, cot_hbm,
    act, igrad, carried, wout,
    rx, rsel, hp, hrx, hs, hgx, hubsum, mr, mrb, mgx, mdx, mdsum,
    la, lat, bt, loc, base, aggs, gps, dg, gs, gx, px, back,
    weight, cot, ws, w1, w2s, w2r, w3s, w3r,
    load_sem, f_send, f_recv, h_send, h_recv, hg_send, hg_recv,
    m_send, m_recv, md_send, md_recv, g_send, g_recv, p_recv,
    w1_send, w1_recv, w2_send, w2_recv, w3_send, w3_recv,
):
    iters, nodes, width, doms, groups, hubdev, orders, cap, scatter, scale = cfg
    half = width // HALVES
    chips = doms // 2
    tiles = width // TILE
    d = lax.axis_index("dom")
    g = lax.axis_index("group")
    c = lax.rem(d, 2)
    z = lax.div(d, 2)
    partner = d + 1 - 2 * c
    hubs = doms * hubdev
    rows8 = iters * hubdev

    load_w = pltpu.make_async_copy(weight_hbm, weight, load_sem.at[0])
    load_c = pltpu.make_async_copy(cot_hbm, cot, load_sem.at[1])
    load_w.start()
    load_c.start()

    barrier = pltpu.get_barrier_semaphore()

    def greet_dom(k, _):
        pl.semaphore_signal(barrier, inc=1, device_id={"dom": lax.rem(d + k, doms)}, device_id_type=MESH)
        return 0

    def greet_group(k, _):
        pl.semaphore_signal(barrier, inc=1, device_id={"group": lax.rem(g + k, groups)}, device_id_type=MESH)
        return 0

    lax.fori_loop(1, doms, greet_dom, 0)
    lax.fori_loop(1, groups, greet_group, 0)

    r = lax.broadcasted_iota(jnp.int32, (doms * rows8, hubs), 0)
    q = lax.broadcasted_iota(jnp.int32, (doms * rows8, hubs), 1)
    spread = []
    for t in range(iters):
        hit = (r // rows8 == q // hubdev) & (r % rows8 == t * hubdev + q % hubdev)
        spread.append(jnp.where(hit, 1.0, 0.0).astype(BF16))
    hub_rows = [mm(spread[t], hub[...]).astype(BF16) for t in range(iters)]

    side = width // 2

    def hub_partial(cols):
        total = mm(hub_rows[0], feats[0, :, cols])
        for t in range(1, iters):
            total = total + mm(hub_rows[t], feats[t, :, cols])
        return total.reshape(doms, rows8, TILE)

    @pl.loop(0, tiles // 2)
    def _(i):
        left = pl.multiple_of(i * TILE, TILE)
        both = jnp.concatenate(
            [hub_partial(pl.ds(left, TILE)), hub_partial(pl.ds(left + side, TILE))], axis=1)
        hp[:, :, pl.ds(left, TILE)] = both.astype(BF16)

    pl.semaphore_wait(barrier, doms + groups - 2)

    def f_copy(kind, b, src, dst_slot, device):
        return pltpu.make_async_remote_copy(
            src_ref=src.at[pl.ds(b * BLK, BLK), :],
            dst_ref=rx.at[dst_slot, pl.ds(b * BLK, BLK), :],
            send_sem=f_send.at[kind, b],
            recv_sem=f_recv.at[dst_slot, b],
            device_id={"dom": device},
            device_id_type=MESH,
        )

    up = d + 2 < doms
    down = d >= 2
    relays = jnp.where(c == 1, d >= 2, d + 2 < doms)
    relayed = jnp.where(c == 1, partner + 2 < doms, partner >= 2)
    own = feats.at[0]
    nb = nodes // BLK
    up_to = jnp.minimum(d + 2, doms - 1)
    down_to = jnp.maximum(d - 2, 0)
    for b in range(nb):
        @pl.when(up)
        def _():
            f_copy(0, b, own, 3, up_to).start()

        @pl.when(down)
        def _():
            f_copy(1, b, own, 2, down_to).start()

    def h_copy(k):
        e = lax.rem(d + k, doms)
        return pltpu.make_async_remote_copy(
            src_ref=hp.at[e], dst_ref=hrx.at[k], send_sem=h_send.at[k], recv_sem=h_recv.at[k],
            device_id={"dom": e}, device_id_type=MESH)

    def each(count, body):
        def step(k, _):
            body(k)
            return 0
        lax.fori_loop(1, count, step, 0)

    each(doms, lambda k: h_copy(k).start())
    for b in range(nb):
        f_copy(2, b, own, 1 - c, partner).start()

    for i in range(nb):
        for j in range(nb):
            m = mask[i, j].astype(F32)
            la[i * BLK:(i + 1) * BLK, j * BLK:(j + 1) * BLK] = (
                adj[i * BLK:(i + 1) * BLK, j * BLK:(j + 1) * BLK].astype(F32) * m
            ).astype(BF16)
    lat[...] = la[...].T
    for o in range(orders):
        bt[o * cap * BLK:(o + 1) * cap * BLK, :] = badj[:, o * cap * BLK:(o + 1) * cap * BLK].T

    @pl.loop(0, tiles)
    def _(i):
        cols = pl.ds(pl.multiple_of(i * TILE, TILE), TILE)
        for t in range(iters):
            loc[t, :, cols] = mm(la[...], feats[t, :, cols])

    def add_h(k, total):
        h_copy(k).wait_recv()
        return total + hrx[k].astype(F32)

    hs[...] = lax.fori_loop(1, doms, add_h, hp[d].astype(F32))

    def hg_copy(k):
        e = lax.rem(g + k, groups)
        return pltpu.make_async_remote_copy(
            src_ref=hs, dst_ref=hgx.at[k], send_sem=hg_send.at[k], recv_sem=hg_recv.at[k],
            device_id={"group": e}, device_id_type=MESH)

    each(groups, lambda k: hg_copy(k).start())

    for b in range(nb):
        @pl.when(relays)
        def _():
            f_copy(0, b, own, 2 + c, partner).wait_recv()
            f_copy(3, b, rx.at[2 + c], c, partner).start()

    def pick(o):
        for j in range(cap):
            want = bblocks[0, o, j, d]
            m0 = (want == 0).astype(F32)
            m1 = (want == 1).astype(F32)
            start = (o * cap + j) * BLK
            rsel[start:start + BLK, :] = (
                rx[o, 0:BLK, :].astype(F32) * m0 + rx[o, BLK:2 * BLK, :].astype(F32) * m1
            ).astype(BF16)

    def wait_slot(o):
        for b in range(nb):
            f_copy(0, b, own, o, partner).wait_recv()

    for o in (0, 1):
        first = jnp.where(c == o, True, relayed)
        @pl.when(first)
        def _():
            wait_slot(o)
            pick(o)

        @pl.when(jnp.logical_not(first))
        def _():
            rsel[o * cap * BLK:(o + 1) * cap * BLK, :] = jnp.zeros((cap * BLK, width), BF16)

    for o, there in ((2, up), (3, down)):
        @pl.when(there)
        def _():
            @pl.when(c != o - 2)
            def _():
                wait_slot(o)
            pick(o)

        @pl.when(jnp.logical_not(there))
        def _():
            rsel[o * cap * BLK:(o + 1) * cap * BLK, :] = jnp.zeros((cap * BLK, width), BF16)

    @pl.loop(0, tiles)
    def _(i):
        cols = pl.ds(pl.multiple_of(i * TILE, TILE), TILE)
        base[:, cols] = mm(badj[...], rsel[:, cols])

    def add_hg(k, total):
        hg_copy(k).wait_recv()
        return total + hgx[k]

    hub_all = lax.fori_loop(1, groups, add_hg, hs[...])
    hubsum[:, 0:side] = hub_all[0:rows8]
    hubsum[:, side:width] = hub_all[rows8:2 * rows8]
    load_w.wait()
    load_c.wait()

    stride = nodes // hubdev
    spot = lax.broadcasted_iota(jnp.int32, (stride, TILE), 0)

    order_of = (1 - c, 3 - c, c, 2 + c)
    reach1 = jnp.where(c == 1, d + 2 < doms, d >= 2)

    def aside(order):
        return jnp.clip(d + 2 * (5 - 2 * order), 0, doms - 1)

    def g_copy(t, kind):
        if kind == 0:
            dst, sem, to = px.at[t], p_recv.at[t], partner
        else:
            slot = 0 if kind == 2 else 4 - order_of[kind]
            dst, sem = gx.at[t, slot], g_recv.at[t, slot]
            to = partner if kind == 2 else aside(order_of[kind])
        return pltpu.make_async_remote_copy(
            src_ref=gs.at[t, kind], dst_ref=dst, send_sem=g_send.at[t, kind], recv_sem=sem,
            device_id={"dom": to}, device_id_type=MESH)

    def g_wait(t, slot):
        pltpu.make_async_remote_copy(
            src_ref=gs.at[t, 0], dst_ref=gx.at[t, slot], send_sem=g_send.at[t, 0], recv_sem=g_recv.at[t, slot],
            device_id={"dom": partner}, device_id_type=MESH).wait_recv()

    def folded(t, kind, put):
        o = order_of[kind]
        slots = pl.ds(pl.multiple_of(o * cap * BLK, cap * BLK), cap * BLK)
        asked = [bblocks[0, o, j, d] for j in range(cap)]

        @pl.loop(0, tiles)
        def _(i):
            cols = pl.ds(pl.multiple_of(i * TILE, TILE), TILE)
            grad = mm(bt[slots, :], dg[t, :, cols]).astype(BF16).astype(F32)
            for b in range(nb):
                total = grad[0:BLK] * (asked[0] == b).astype(F32)
                for j in range(1, cap):
                    total = total + grad[j * BLK:(j + 1) * BLK] * (asked[j] == b).astype(F32)
                put(b, cols, total)

    def send_plain(t):
        for kind, when in ((0, relayed), (1, reach1), (2, None)):
            def put(b, cols, total, kind=kind):
                gs[t, kind, b * BLK:(b + 1) * BLK, cols] = total.astype(BF16)
            folded(t, kind, put)
            if when is None:
                g_copy(t, kind).start()
            else:
                @pl.when(when)
                def _():
                    g_copy(t, kind).start()

    def send_joined(t):
        @pl.when(relays)
        def _():
            g_copy(t, 0).wait_recv()

            def put(b, cols, total):
                rows = slice(b * BLK, (b + 1) * BLK)
                gs[t, 3, rows, cols] = (total + px[t, rows, cols].astype(F32)).astype(BF16)
            folded(t, 3, put)
            g_copy(t, 3).start()

    def md_copy(k):
        e = lax.rem(d + k, doms)
        return pltpu.make_async_remote_copy(
            src_ref=mrb, dst_ref=mdx.at[d], send_sem=md_send.at[k], recv_sem=md_recv.at[k],
            device_id={"dom": e}, device_id_type=MESH)

    def m_copy(k):
        e = lax.rem(g + k, groups)
        return pltpu.make_async_remote_copy(
            src_ref=mdx, dst_ref=mgx.at[k], send_sem=m_send.at[k], recv_sem=m_recv.at[k],
            device_id={"group": e}, device_id_type=MESH)

    for t in range(iters):
        lo = t * nodes

        @pl.loop(0, tiles)
        def _(i):
            cols = pl.ds(pl.multiple_of(i * TILE, TILE), TILE)
            for k in range(hubdev):
                part = slice(k * stride, (k + 1) * stride)
                total = loc[t, part, cols] + base[part, cols]
                add = jnp.where(spot == offs[0, k], hubsum[t * hubdev + k:t * hubdev + k + 1, cols], 0.0)
                aggs[lo + k * stride:lo + (k + 1) * stride, cols] = (total + add).astype(BF16)

        @pl.loop(0, tiles)
        def _(i):
            cols = pl.ds(pl.multiple_of(i * TILE, TILE), TILE)
            pre = mm_nt(aggs[lo:lo + nodes, :], weight[cols, :])
            sig = 1.0 / (1.0 + jnp.exp(-pre))
            act[t, :, cols] = (pre * sig).astype(BF16)
            gps[lo:lo + nodes, cols] = (
                cot[t, :, cols].astype(F32) * sig * (1.0 + pre * (1.0 - sig))).astype(BF16)

        @pl.loop(0, tiles)
        def _(i):
            cols = pl.ds(pl.multiple_of(i * TILE, TILE), TILE)
            dagg = mm(gps[lo:lo + nodes, :], weight[:, cols]).astype(BF16)
            dg[t, :, cols] = dagg
            for k in range(hubdev):
                rows = dagg[k * stride:(k + 1) * stride, :].astype(F32)
                hit = jnp.where(spot == offs[0, k], rows, 0.0)
                mr[t * hubdev + k:t * hubdev + k + 1, cols] = jnp.sum(hit, axis=0, keepdims=True)

        if t > 0:
            send_joined(t - 1)
        if t + 1 == iters:
            mrb[0:rows8, :] = mr[:, 0:side].astype(BF16)
            mrb[rows8:2 * rows8, :] = mr[:, side:width].astype(BF16)
            each(doms, lambda k: md_copy(k).start())
        send_plain(t)

    devices = doms * groups
    if scatter:
        rows = width // devices
        per = BLK // rows

        def w1_copy(h):
            return pltpu.make_async_remote_copy(
                src_ref=ws.at[h, 1 - c], dst_ref=w1.at[h], send_sem=w1_send.at[h], recv_sem=w1_recv.at[h],
                device_id={"dom": partner}, device_id_type=MESH)

        for h in range(HALVES):
            @pl.loop(0, width // BLK)
            def _(i):
                lhs = gps[:, pl.ds(pl.multiple_of(i * BLK, BLK), BLK)]
                res = mm_tn(lhs, aggs[:, h * half:(h + 1) * half]).astype(BF16)
                for p in range(per):
                    f = i * per + p
                    ws[h, p % 2, f // 2] = res[p * rows:(p + 1) * rows, :]
            w1_copy(h).start()
    else:
        @pl.loop(0, width // BLK)
        def _(i):
            at = pl.ds(pl.multiple_of(i * BLK, BLK), BLK)
            wout[at, :] = mm_tn(gps[:, at], aggs[...])

    @pl.loop(0, tiles)
    def _(i):
        cols = pl.ds(pl.multiple_of(i * TILE, TILE), TILE)
        for t in range(iters):
            loc[t, :, cols] = mm(lat[...], dg[t, :, cols])

    send_joined(iters - 1)

    mdx[d] = mrb[...]
    each(doms, lambda k: pltpu.make_async_remote_copy(
        src_ref=mrb, dst_ref=mdx.at[lax.rem(d + doms - k, doms)], send_sem=md_send.at[k], recv_sem=md_recv.at[k],
        device_id={"dom": partner}, device_id_type=MESH).wait_recv())
    each(groups, lambda k: m_copy(k).start())

    if scatter:
        def w2_copy(h, k):
            e = lax.rem(g + k, groups)
            return pltpu.make_async_remote_copy(
                src_ref=w2s.at[h, pl.ds(e * chips, chips)], dst_ref=w2r.at[h, k],
                send_sem=w2_send.at[h, k], recv_sem=w2_recv.at[h, k],
                device_id={"group": e}, device_id_type=MESH)

        def w3_copy(h, k):
            e = lax.rem(z + k, chips)
            return pltpu.make_async_remote_copy(
                src_ref=w3s.at[h, e], dst_ref=w3r.at[h, k],
                send_sem=w3_send.at[h, k], recv_sem=w3_recv.at[h, k],
                device_id={"dom": e * 2 + c}, device_id_type=MESH)

        for h in range(HALVES):
            w1_copy(h).wait_recv()

            @pl.loop(0, groups * chips)
            def _(i):
                w2s[h, i] = (ws[h, c, i].astype(F32) + w1[h, i].astype(F32)).astype(BF16)
            for k in range(1, groups):
                w2_copy(h, k).start()

        for h in range(HALVES):
            for k in range(1, groups):
                w2_copy(h, k).wait_recv()

            @pl.loop(0, chips)
            def _(i):
                total = w2s[h, g * chips + i].astype(F32)
                for k in range(1, groups):
                    total = total + w2r[h, k, i].astype(F32)
                w3s[h, i] = total.astype(BF16)
            each(chips, lambda k: w3_copy(h, k).start())

    each(groups, lambda k: m_copy(k).wait_recv())
    total = mdx[...].astype(F32)
    for k in range(1, groups):
        total = total + mgx[k].astype(F32)
    mdsum[...] = total
    hub_cols = [
        lax.dot_general(hub[...], spread[t], (((0,), (1,)), ((), ())), preferred_element_type=F32).astype(BF16)
        for t in range(iters)]

    def add_hubs(first, lo_col, i):
        inner = pl.ds(pl.multiple_of(i * TILE, TILE), TILE)
        cols = pl.ds(pl.multiple_of(lo_col + i * TILE, TILE), TILE)
        piece = mdsum[:, first:first + rows8, inner].reshape(doms * rows8, TILE)
        upper = piece.astype(BF16)
        lower = (piece - upper.astype(F32)).astype(BF16)
        for t in range(iters):
            total = loc[t, :, cols] + mm(hub_cols[t], upper) + mm(hub_cols[t], lower)
            if t == 0:
                igrad[0, :, cols] = total.astype(BF16)
            else:
                loc[t, :, cols] = total

    for part in range(2):
        pl.loop(0, tiles // 2)(functools.partial(add_hubs, part * rows8, part * side))

    for t in range(iters):
        g_wait(t, 0)
        if t + 1 < iters:
            loc[t + 1] += gx[t, 0].astype(F32)
            acc = loc.at[t + 1]
        else:
            back[...] = gx[t, 0].astype(F32)
            acc = back
        for slot, there in ((1, up), (2, down)):
            @pl.when(there)
            def _():
                g_wait(t, slot)
                acc[...] += gx[t, slot].astype(F32)
        if t + 1 < iters:
            igrad[t + 1] = acc[...].astype(BF16)
        else:
            carried[...] = acc[...].astype(BF16)

    if scatter:
        for h in range(HALVES):
            each(chips, lambda k: w3_copy(h, k).wait_recv())
            total = w3s[h, z].astype(F32)
            for k in range(1, chips):
                total = total + w3r[h, k].astype(F32)
            wout[:, h * half:(h + 1) * half] = total * scale

    for b in range(nb):
        @pl.when(up)
        def _():
            f_copy(0, b, own, 3, up_to).wait_send()

        @pl.when(down)
        def _():
            f_copy(1, b, own, 2, down_to).wait_send()

        f_copy(2, b, own, 1 - c, partner).wait_send()

        @pl.when(relays)
        def _():
            f_copy(3, b, rx.at[2 + c], c, partner).wait_send()
    each(doms, lambda k: h_copy(k).wait_send())
    each(groups, lambda k: hg_copy(k).wait_send())
    each(groups, lambda k: m_copy(k).wait_send())
    each(doms, lambda k: md_copy(k).wait_send())
    for t in range(iters):
        for kind, when in ((0, relayed), (1, reach1), (3, relays)):
            @pl.when(when)
            def _():
                g_copy(t, kind).wait_send()
        g_copy(t, 2).wait_send()
    if scatter:
        for h in range(HALVES):
            w1_copy(h).wait_send()
            for k in range(1, groups):
                w2_copy(h, k).wait_send()
            each(chips, lambda k: w3_copy(h, k).wait_send())


def per_device(features, adjacency, tile_mask, boundary_adj, boundary_blocks, hub_adj, hub_offsets, weight, cotangent):
    iters, nodes, width = features.shape
    orders, cap = boundary_blocks.shape[2:]
    doms = lax.axis_size("dom")
    groups = lax.axis_size("group")
    devices = doms * groups
    hubdev = hub_offsets.shape[1]
    chips = doms // 2
    rows = width // devices
    rows8 = iters * hubdev
    half = width // HALVES
    scatter = rows % 16 == 0 and BLK % (2 * rows) == 0
    scale = (iters * nodes * devices) ** (-0.5)
    cfg = (iters, nodes, width, doms, groups, hubdev, orders, cap, scatter, scale)
    dma = pltpu.SemaphoreType.DMA
    vmem = pltpu.VMEM
    wshape = (rows, half) if scatter else (16, 128)
    wide = groups * chips if scatter else 1
    deep = chips if scatter else 1
    packed = (2 * rows8, width // 2)
    scratch = [
        vmem((orders, nodes, width), BF16),
        vmem((orders * cap * BLK, width), BF16),
        vmem((doms,) + packed, BF16),
        vmem((doms,) + packed, BF16),
        vmem(packed, F32),
        vmem((groups,) + packed, F32),
        vmem((rows8, width), F32),
        vmem((rows8, width), F32),
        vmem(packed, BF16),
        vmem((groups, doms) + packed, BF16),
        vmem((doms,) + packed, BF16),
        vmem((doms,) + packed, F32),
        vmem((nodes, nodes), BF16),
        vmem((nodes, nodes), BF16),
        vmem((orders * cap * BLK, nodes), BF16),
        vmem((iters, nodes, width), F32),
        vmem((nodes, width), F32),
        vmem((iters * nodes, width), BF16),
        vmem((iters * nodes, width), BF16),
        vmem((iters, nodes, width), BF16),
        vmem((iters, 4, nodes, width), BF16),
        vmem((iters, 3, nodes, width), BF16),
        vmem((iters, nodes, width), BF16),
        vmem((nodes, width), F32),
        vmem(weight.shape, BF16),
        vmem(cotangent.shape, BF16),
        vmem((HALVES, 2, wide) + wshape, BF16),
        vmem((HALVES, wide) + wshape, BF16),
        vmem((HALVES, wide) + wshape, BF16),
        vmem((HALVES, groups, deep) + wshape, BF16),
        vmem((HALVES, deep) + wshape, BF16),
        vmem((HALVES, deep) + wshape, BF16),
        dma((2,)), dma((4, nodes // BLK)), dma((4, nodes // BLK)),
        dma((doms,)), dma((doms,)), dma((groups,)), dma((groups,)),
        dma((groups,)), dma((groups,)), dma((doms,)), dma((doms,)),
        dma((iters, 4)), dma((iters, 3)), dma((iters,)),
        dma((HALVES,)), dma((HALVES,)), dma((HALVES, groups)), dma((HALVES, groups)),
        dma((HALVES, chips)), dma((HALVES, chips)),
    ]
    in_vmem = pl.BlockSpec(memory_space=pltpu.VMEM)
    in_smem = pl.BlockSpec(memory_space=pltpu.SMEM)
    anywhere = pl.BlockSpec(memory_space=pltpu.MemorySpace.HBM)
    act, igrad, carried, wgrad = pl.pallas_call(
        functools.partial(kernel, cfg),
        out_shape=(
            jax.ShapeDtypeStruct(features.shape, BF16),
            jax.ShapeDtypeStruct(features.shape, BF16),
            jax.ShapeDtypeStruct((nodes, width), BF16),
            jax.ShapeDtypeStruct((rows if scatter else width, width), F32),
        ),
        in_specs=[in_vmem, in_vmem, in_smem, in_vmem, in_smem, in_vmem, in_smem, anywhere, anywhere],
        out_specs=(in_vmem,) * 4,
        scratch_shapes=scratch,
        compiler_params=pltpu.CompilerParams(
            collective_id=0, has_side_effects=True, vmem_limit_bytes=44 * 1024 * 1024),
        cost_estimate=pl.CostEstimate(flops=6 * 10**9, bytes_accessed=10**7, transcendentals=10**6),
    )(features, adjacency, tile_mask, boundary_adj, boundary_blocks.transpose(0, 2, 3, 1), hub_adj, hub_offsets, weight, cotangent)
    if not scatter:
        wgrad = scale * lax.psum_scatter(wgrad, ("group", "dom"), scatter_dimension=0, tiled=True)
    return act, igrad, carried, wgrad


def solution(mesh):
    return jax.shard_map(
        per_device,
        mesh=mesh,
        in_specs=(
            P(None, ("group", "dom"), None),
            P(("group", "dom"), None),
            P(("group", "dom"), None),
            P(("group", "dom"), None),
            P("group", None, None, None),
            P(None, ("group", "dom")),
            P("group", "dom"),
            P(),
            P(None, ("group", "dom"), None),
        ),
        out_specs=(
            P(None, ("group", "dom"), None),
            P(None, ("group", "dom"), None),
            P(("group", "dom"), None),
            P(("group", "dom"), None),
        ),
        check_vma=False,
    )
```

```python
import functools

import jax
import jax.numpy as jnp
from jax import lax
from jax.experimental import pallas as pl
from jax.experimental.pallas import tpu as pltpu
from jax.sharding import PartitionSpec as P

BLK = 128
TILE = 256
HALVES = 2
MESH = pl.DeviceIdType.MESH
F32 = jnp.float32
BF16 = jnp.bfloat16


def offset_of(order):
    return (order // 2 + 1) * (1 - 2 * (order % 2))


def mm(left, right):
    return jnp.dot(left, right, preferred_element_type=F32)


def mm_nt(left, right):
    return lax.dot_general(left, right, (((1,), (1,)), ((), ())), preferred_element_type=F32)


def mm_tn(left, right):
    return lax.dot_general(left, right, (((0,), (0,)), ((), ())), preferred_element_type=F32)


def kernel(
    cfg,
    feats, adj, mask, badj, bblocks, hub, offs, weight_hbm, cot_hbm,
    act, igrad, carried, wout,
    rx, rsel, hp, hrx, hs, hgx, hubsum, mr, mrb, mgx, mdx, mdsum,
    la, lat, bt, loc, base, aggs, gps, gpt, dg, gs, gx, px, back,
    weight, cot, ws, w1, w2s, w2r, w3s, w3r,
    load_sem, f_send, f_recv, h_send, h_recv, hg_send, hg_recv,
    m_send, m_recv, md_send, md_recv, g_send, g_recv, p_recv,
    w1_send, w1_recv, w2_send, w2_recv, w3_send, w3_recv,
):
    iters, nodes, width, doms, groups, hubdev, orders, cap, scatter, scale = cfg
    half = width // HALVES
    chips = doms // 2
    tiles = width // TILE
    d = lax.axis_index("dom")
    g = lax.axis_index("group")
    c = lax.rem(d, 2)
    z = lax.div(d, 2)
    partner = d + 1 - 2 * c
    hubs = doms * hubdev
    rows8 = iters * hubdev

    load_w = pltpu.make_async_copy(weight_hbm, weight, load_sem.at[0])
    load_c = pltpu.make_async_copy(cot_hbm, cot, load_sem.at[1])
    load_w.start()
    load_c.start()

    barrier = pltpu.get_barrier_semaphore()

    def greet_dom(k, _):
        pl.semaphore_signal(barrier, inc=1, device_id={"dom": lax.rem(d + k, doms)}, device_id_type=MESH)
        return 0

    def greet_group(k, _):
        pl.semaphore_signal(barrier, inc=1, device_id={"group": lax.rem(g + k, groups)}, device_id_type=MESH)
        return 0

    lax.fori_loop(1, doms, greet_dom, 0)
    lax.fori_loop(1, groups, greet_group, 0)

    r = lax.broadcasted_iota(jnp.int32, (doms * rows8, hubs), 0)
    q = lax.broadcasted_iota(jnp.int32, (doms * rows8, hubs), 1)
    spread = []
    for t in range(iters):
        hit = (r // rows8 == q // hubdev) & (r % rows8 == t * hubdev + q % hubdev)
        spread.append(jnp.where(hit, 1.0, 0.0).astype(BF16))
    hub_rows = [mm(spread[t], hub[...]).astype(BF16) for t in range(iters)]

    pl.semaphore_wait(barrier, doms + groups - 2)

    def f_copy(kind, b, src, dst_slot, device):
        return pltpu.make_async_remote_copy(
            src_ref=src.at[pl.ds(b * BLK, BLK), :],
            dst_ref=rx.at[dst_slot, pl.ds(b * BLK, BLK), :],
            send_sem=f_send.at[kind, b],
            recv_sem=f_recv.at[dst_slot, b],
            device_id={"dom": device},
            device_id_type=MESH,
        )

    up = d + 2 < doms
    down = d >= 2
    relays = jnp.where(c == 1, d >= 2, d + 2 < doms)
    relayed = jnp.where(c == 1, partner + 2 < doms, partner >= 2)
    own = feats.at[0]
    nb = nodes // BLK
    up_to = jnp.minimum(d + 2, doms - 1)
    down_to = jnp.maximum(d - 2, 0)
    for b in range(nb):
        @pl.when(up)
        def _():
            f_copy(0, b, own, 3, up_to).start()

        @pl.when(down)
        def _():
            f_copy(1, b, own, 2, down_to).start()

    for b in range(nb):
        f_copy(2, b, own, 1 - c, partner).start()

    side = width // 2

    def hub_partial(cols):
        total = mm(hub_rows[0], feats[0, :, cols])
        for t in range(1, iters):
            total = total + mm(hub_rows[t], feats[t, :, cols])
        return total.reshape(doms, rows8, TILE)

    @pl.loop(0, tiles // 2)
    def _(i):
        left = pl.multiple_of(i * TILE, TILE)
        both = jnp.concatenate(
            [hub_partial(pl.ds(left, TILE)), hub_partial(pl.ds(left + side, TILE))], axis=1)
        hp[:, :, pl.ds(left, TILE)] = both.astype(BF16)

    def h_copy(k):
        e = lax.rem(d + k, doms)
        return pltpu.make_async_remote_copy(
            src_ref=hp.at[e], dst_ref=hrx.at[k], send_sem=h_send.at[k], recv_sem=h_recv.at[k],
            device_id={"dom": e}, device_id_type=MESH)

    def each(count, body):
        def step(k, _):
            body(k)
            return 0
        lax.fori_loop(1, count, step, 0)

    each(doms, lambda k: h_copy(k).start())
    for i in range(nb):
        for j in range(nb):
            m = mask[i, j].astype(F32)
            la[i * BLK:(i + 1) * BLK, j * BLK:(j + 1) * BLK] = (
                adj[i * BLK:(i + 1) * BLK, j * BLK:(j + 1) * BLK].astype(F32) * m
            ).astype(BF16)
    lat[...] = la[...].T
    for o in range(orders):
        bt[o * cap * BLK:(o + 1) * cap * BLK, :] = badj[:, o * cap * BLK:(o + 1) * cap * BLK].T

    @pl.loop(0, tiles)
    def _(i):
        cols = pl.ds(pl.multiple_of(i * TILE, TILE), TILE)
        for t in range(iters):
            loc[t, :, cols] = mm(la[...], feats[t, :, cols])

    def add_h(k, total):
        h_copy(k).wait_recv()
        return total + hrx[k].astype(F32)

    hs[...] = lax.fori_loop(1, doms, add_h, hp[d].astype(F32))

    def hg_copy(k):
        e = lax.rem(g + k, groups)
        return pltpu.make_async_remote_copy(
            src_ref=hs, dst_ref=hgx.at[k], send_sem=hg_send.at[k], recv_sem=hg_recv.at[k],
            device_id={"group": e}, device_id_type=MESH)

    each(groups, lambda k: hg_copy(k).start())

    for b in range(nb):
        @pl.when(relays)
        def _():
            f_copy(0, b, own, 2 + c, partner).wait_recv()
            f_copy(3, b, rx.at[2 + c], c, partner).start()

    def pick(o):
        for j in range(cap):
            want = bblocks[0, o, j, d]
            m0 = (want == 0).astype(F32)
            m1 = (want == 1).astype(F32)
            start = (o * cap + j) * BLK
            rsel[start:start + BLK, :] = (
                rx[o, 0:BLK, :].astype(F32) * m0 + rx[o, BLK:2 * BLK, :].astype(F32) * m1
            ).astype(BF16)

    def wait_slot(o):
        for b in range(nb):
            f_copy(0, b, own, o, partner).wait_recv()

    for o in (0, 1):
        first = jnp.where(c == o, True, relayed)
        @pl.when(first)
        def _():
            wait_slot(o)
            pick(o)

        @pl.when(jnp.logical_not(first))
        def _():
            rsel[o * cap * BLK:(o + 1) * cap * BLK, :] = jnp.zeros((cap * BLK, width), BF16)

    for o, there in ((2, up), (3, down)):
        @pl.when(there)
        def _():
            @pl.when(c != o - 2)
            def _():
                wait_slot(o)
            pick(o)

        @pl.when(jnp.logical_not(there))
        def _():
            rsel[o * cap * BLK:(o + 1) * cap * BLK, :] = jnp.zeros((cap * BLK, width), BF16)

    @pl.loop(0, tiles)
    def _(i):
        cols = pl.ds(pl.multiple_of(i * TILE, TILE), TILE)
        base[:, cols] = mm(badj[...], rsel[:, cols])

    def add_hg(k, total):
        hg_copy(k).wait_recv()
        return total + hgx[k]

    hub_all = lax.fori_loop(1, groups, add_hg, hs[...])
    hubsum[:, 0:side] = hub_all[0:rows8]
    hubsum[:, side:width] = hub_all[rows8:2 * rows8]
    load_w.wait()
    load_c.wait()

    stride = nodes // hubdev
    spot = lax.broadcasted_iota(jnp.int32, (stride, TILE), 0)

    order_of = (1 - c, 3 - c, c, 2 + c)
    reach1 = jnp.where(c == 1, d + 2 < doms, d >= 2)

    def aside(order):
        return jnp.clip(d + 2 * (5 - 2 * order), 0, doms - 1)

    def g_copy(t, kind):
        if kind == 0:
            dst, sem, to = px.at[t], p_recv.at[t], partner
        else:
            slot = 0 if kind == 2 else 4 - order_of[kind]
            dst, sem = gx.at[t, slot], g_recv.at[t, slot]
            to = partner if kind == 2 else aside(order_of[kind])
        return pltpu.make_async_remote_copy(
            src_ref=gs.at[t, kind], dst_ref=dst, send_sem=g_send.at[t, kind], recv_sem=sem,
            device_id={"dom": to}, device_id_type=MESH)

    def g_wait(t, slot):
        pltpu.make_async_remote_copy(
            src_ref=gs.at[t, 0], dst_ref=gx.at[t, slot], send_sem=g_send.at[t, 0], recv_sem=g_recv.at[t, slot],
            device_id={"dom": partner}, device_id_type=MESH).wait_recv()

    def folded(t, kind, put):
        o = order_of[kind]
        slots = pl.ds(pl.multiple_of(o * cap * BLK, cap * BLK), cap * BLK)
        asked = [bblocks[0, o, j, d] for j in range(cap)]

        @pl.loop(0, tiles)
        def _(i):
            cols = pl.ds(pl.multiple_of(i * TILE, TILE), TILE)
            grad = mm(bt[slots, :], dg[t, :, cols]).astype(BF16).astype(F32)
            for b in range(nb):
                total = grad[0:BLK] * (asked[0] == b).astype(F32)
                for j in range(1, cap):
                    total = total + grad[j * BLK:(j + 1) * BLK] * (asked[j] == b).astype(F32)
                put(b, cols, total)

    def send_plain(t):
        for kind, when in ((0, relayed), (1, reach1), (2, None)):
            def put(b, cols, total, kind=kind):
                gs[t, kind, b * BLK:(b + 1) * BLK, cols] = total.astype(BF16)
            folded(t, kind, put)
            if when is None:
                g_copy(t, kind).start()
            else:
                @pl.when(when)
                def _():
                    g_copy(t, kind).start()

    def send_joined(t):
        @pl.when(relays)
        def _():
            g_copy(t, 0).wait_recv()

            def put(b, cols, total):
                rows = slice(b * BLK, (b + 1) * BLK)
                gs[t, 3, rows, cols] = (total + px[t, rows, cols].astype(F32)).astype(BF16)
            folded(t, 3, put)
            g_copy(t, 3).start()

    def md_copy(k):
        e = lax.rem(d + k, doms)
        return pltpu.make_async_remote_copy(
            src_ref=mrb, dst_ref=mdx.at[d], send_sem=md_send.at[k], recv_sem=md_recv.at[k],
            device_id={"dom": e}, device_id_type=MESH)

    def m_copy(k):
        e = lax.rem(g + k, groups)
        return pltpu.make_async_remote_copy(
            src_ref=mdx, dst_ref=mgx.at[k], send_sem=m_send.at[k], recv_sem=m_recv.at[k],
            device_id={"group": e}, device_id_type=MESH)

    @pl.loop(0, tiles)
    def _(i):
        cols = pl.ds(pl.multiple_of(i * TILE, TILE), TILE)
        for k in range(hubdev):
            part = slice(k * stride, (k + 1) * stride)
            hit = spot == offs[0, k]
            for t in range(iters):
                lo = t * nodes + k * stride
                total = loc[t, part, cols] + base[part, cols]
                add = jnp.where(hit, hubsum[t * hubdev + k:t * hubdev + k + 1, cols], 0.0)
                aggs[lo:lo + stride, cols] = (total + add).astype(BF16)

    @pl.loop(0, tiles)
    def _(i):
        cols = pl.ds(pl.multiple_of(i * TILE, TILE), TILE)
        pre_all = mm_nt(aggs[...], weight[cols, :])
        for t in range(iters):
            lo = t * nodes
            pre = pre_all[lo:lo + nodes]
            sig = 1.0 / (1.0 + jnp.exp(-pre))
            act[t, :, cols] = (pre * sig).astype(BF16)
            gps[lo:lo + nodes, cols] = (
                cot[t, :, cols].astype(F32) * sig * (1.0 + pre * (1.0 - sig))).astype(BF16)

    @pl.loop(0, tiles)
    def _(i):
        cols = pl.ds(pl.multiple_of(i * TILE, TILE), TILE)
        dagg = mm(gps[...], weight[:, cols]).astype(BF16)
        for t in range(iters):
            dg[t, :, cols] = dagg[t * nodes:(t + 1) * nodes]
            for k in range(hubdev):
                lo = t * nodes + k * stride
                hit = jnp.where(spot == offs[0, k], dagg[lo:lo + stride, :].astype(F32), 0.0)
                mr[t * hubdev + k:t * hubdev + k + 1, cols] = jnp.sum(hit, axis=0, keepdims=True)

    devices = doms * groups
    rows = width // devices

    def w1_copy(h):
        return pltpu.make_async_remote_copy(
            src_ref=ws.at[h, 1 - c], dst_ref=w1.at[h], send_sem=w1_send.at[h], recv_sem=w1_recv.at[h],
            device_id={"dom": partner}, device_id_type=MESH)

    def w2_copy(h, k):
        e = lax.rem(g + k, groups)
        return pltpu.make_async_remote_copy(
            src_ref=w2s.at[h, pl.ds(e * chips, chips)], dst_ref=w2r.at[h, k],
            send_sem=w2_send.at[h, k], recv_sem=w2_recv.at[h, k],
            device_id={"group": e}, device_id_type=MESH)

    def w3_copy(h, k):
        e = lax.rem(z + k, chips)
        return pltpu.make_async_remote_copy(
            src_ref=w3s.at[h, e], dst_ref=w3r.at[h, k],
            send_sem=w3_send.at[h, k], recv_sem=w3_recv.at[h, k],
            device_id={"dom": e * 2 + c}, device_id_type=MESH)

    def weight_out():
        if scatter:
            for t in range(iters):
                gpt[:, t * nodes:(t + 1) * nodes] = gps[t * nodes:(t + 1) * nodes, :].T

            for h in range(HALVES):
                @pl.loop(0, half // TILE)
                def _(i):
                    inner = pl.ds(pl.multiple_of(i * TILE, TILE), TILE)
                    cols = pl.ds(pl.multiple_of(h * half + i * TILE, TILE), TILE)
                    res = mm(gpt[...], aggs[:, cols]).reshape(groups * chips, 2, rows, TILE).astype(BF16)
                    for p in range(2):
                        ws[h, p, :, :, inner] = res[:, p]
                w1_copy(h).start()
        else:
            @pl.loop(0, width // BLK)
            def _(i):
                at = pl.ds(pl.multiple_of(i * BLK, BLK), BLK)
                wout[at, :] = mm_tn(gps[:, at], aggs[...])

    def weight_on():
        for h in range(HALVES):
            w1_copy(h).wait_recv()

            @pl.loop(0, groups * chips)
            def _(i):
                w2s[h, i] = (ws[h, c, i].astype(F32) + w1[h, i].astype(F32)).astype(BF16)
            for k in range(1, groups):
                w2_copy(h, k).start()

    for t in range(iters):
        if t == 1:
            weight_out()
        if t > 0:
            send_joined(t - 1)
        if t + 1 == iters:
            mrb[0:rows8, :] = mr[:, 0:side].astype(BF16)
            mrb[rows8:2 * rows8, :] = mr[:, side:width].astype(BF16)
            each(doms, lambda k: md_copy(k).start())
        send_plain(t)

    if iters == 1:
        weight_out()
    if scatter:
        weight_on()
    send_joined(iters - 1)

    @pl.loop(0, tiles)
    def _(i):
        cols = pl.ds(pl.multiple_of(i * TILE, TILE), TILE)
        for t in range(iters):
            loc[t, :, cols] = mm(lat[...], dg[t, :, cols])


    mdx[d] = mrb[...]
    each(doms, lambda k: pltpu.make_async_remote_copy(
        src_ref=mrb, dst_ref=mdx.at[lax.rem(d + doms - k, doms)], send_sem=md_send.at[k], recv_sem=md_recv.at[k],
        device_id={"dom": partner}, device_id_type=MESH).wait_recv())
    each(groups, lambda k: m_copy(k).start())

    if scatter:
        for h in range(HALVES):
            for k in range(1, groups):
                w2_copy(h, k).wait_recv()

            @pl.loop(0, chips)
            def _(i):
                total = w2s[h, g * chips + i].astype(F32)
                for k in range(1, groups):
                    total = total + w2r[h, k, i].astype(F32)
                w3s[h, i] = total.astype(BF16)
            each(chips, lambda k: w3_copy(h, k).start())

    each(groups, lambda k: m_copy(k).wait_recv())
    total = mdx[...].astype(F32)
    for k in range(1, groups):
        total = total + mgx[k].astype(F32)
    mdsum[...] = total
    hub_cols = [
        lax.dot_general(hub[...], spread[t], (((0,), (1,)), ((), ())), preferred_element_type=F32).astype(BF16)
        for t in range(iters)]

    def add_hubs(first, lo_col, i):
        inner = pl.ds(pl.multiple_of(i * TILE, TILE), TILE)
        cols = pl.ds(pl.multiple_of(lo_col + i * TILE, TILE), TILE)
        piece = mdsum[:, first:first + rows8, inner].reshape(doms * rows8, TILE)
        upper = piece.astype(BF16)
        lower = (piece - upper.astype(F32)).astype(BF16)
        for t in range(iters):
            total = loc[t, :, cols] + mm(hub_cols[t], upper) + mm(hub_cols[t], lower)
            if t == 0:
                igrad[0, :, cols] = total.astype(BF16)
            else:
                loc[t, :, cols] = total

    for part in range(2):
        pl.loop(0, tiles // 2)(functools.partial(add_hubs, part * rows8, part * side))

    for t in range(iters):
        g_wait(t, 0)
        if t + 1 < iters:
            loc[t + 1] += gx[t, 0].astype(F32)
            acc = loc.at[t + 1]
        else:
            back[...] = gx[t, 0].astype(F32)
            acc = back
        for slot, there in ((1, up), (2, down)):
            @pl.when(there)
            def _():
                g_wait(t, slot)
                acc[...] += gx[t, slot].astype(F32)
        if t + 1 < iters:
            igrad[t + 1] = acc[...].astype(BF16)
        else:
            carried[...] = acc[...].astype(BF16)

    if scatter:
        for h in range(HALVES):
            each(chips, lambda k: w3_copy(h, k).wait_recv())
            total = w3s[h, z].astype(F32)
            for k in range(1, chips):
                total = total + w3r[h, k].astype(F32)
            wout[:, h * half:(h + 1) * half] = total * scale

    for b in range(nb):
        @pl.when(up)
        def _():
            f_copy(0, b, own, 3, up_to).wait_send()

        @pl.when(down)
        def _():
            f_copy(1, b, own, 2, down_to).wait_send()

        f_copy(2, b, own, 1 - c, partner).wait_send()

        @pl.when(relays)
        def _():
            f_copy(3, b, rx.at[2 + c], c, partner).wait_send()
    each(doms, lambda k: h_copy(k).wait_send())
    each(groups, lambda k: hg_copy(k).wait_send())
    each(groups, lambda k: m_copy(k).wait_send())
    each(doms, lambda k: md_copy(k).wait_send())
    for t in range(iters):
        for kind, when in ((0, relayed), (1, reach1), (3, relays)):
            @pl.when(when)
            def _():
                g_copy(t, kind).wait_send()
        g_copy(t, 2).wait_send()
    if scatter:
        for h in range(HALVES):
            w1_copy(h).wait_send()
            for k in range(1, groups):
                w2_copy(h, k).wait_send()
            each(chips, lambda k: w3_copy(h, k).wait_send())


def per_device(features, adjacency, tile_mask, boundary_adj, boundary_blocks, hub_adj, hub_offsets, weight, cotangent):
    iters, nodes, width = features.shape
    orders, cap = boundary_blocks.shape[2:]
    doms = lax.axis_size("dom")
    groups = lax.axis_size("group")
    devices = doms * groups
    hubdev = hub_offsets.shape[1]
    chips = doms // 2
    rows = width // devices
    rows8 = iters * hubdev
    half = width // HALVES
    scatter = rows % 16 == 0 and BLK % (2 * rows) == 0
    scale = (iters * nodes * devices) ** (-0.5)
    cfg = (iters, nodes, width, doms, groups, hubdev, orders, cap, scatter, scale)
    dma = pltpu.SemaphoreType.DMA
    vmem = pltpu.VMEM
    wshape = (rows, half) if scatter else (16, 128)
    wide = groups * chips if scatter else 1
    deep = chips if scatter else 1
    packed = (2 * rows8, width // 2)
    scratch = [
        vmem((orders, nodes, width), BF16),
        vmem((orders * cap * BLK, width), BF16),
        vmem((doms,) + packed, BF16),
        vmem((doms,) + packed, BF16),
        vmem(packed, F32),
        vmem((groups,) + packed, F32),
        vmem((rows8, width), F32),
        vmem((rows8, width), F32),
        vmem(packed, BF16),
        vmem((groups, doms) + packed, BF16),
        vmem((doms,) + packed, BF16),
        vmem((doms,) + packed, F32),
        vmem((nodes, nodes), BF16),
        vmem((nodes, nodes), BF16),
        vmem((orders * cap * BLK, nodes), BF16),
        vmem((iters, nodes, width), F32),
        vmem((nodes, width), F32),
        vmem((iters * nodes, width), BF16),
        vmem((iters * nodes, width), BF16),
        vmem((width, iters * nodes), BF16),
        vmem((iters, nodes, width), BF16),
        vmem((iters, 4, nodes, width), BF16),
        vmem((iters, 3, nodes, width), BF16),
        vmem((iters, nodes, width), BF16),
        vmem((nodes, width), F32),
        vmem(weight.shape, BF16),
        vmem(cotangent.shape, BF16),
        vmem((HALVES, 2, wide) + wshape, BF16),
        vmem((HALVES, wide) + wshape, BF16),
        vmem((HALVES, wide) + wshape, BF16),
        vmem((HALVES, groups, deep) + wshape, BF16),
        vmem((HALVES, deep) + wshape, BF16),
        vmem((HALVES, deep) + wshape, BF16),
        dma((2,)), dma((4, nodes // BLK)), dma((4, nodes // BLK)),
        dma((doms,)), dma((doms,)), dma((groups,)), dma((groups,)),
        dma((groups,)), dma((groups,)), dma((doms,)), dma((doms,)),
        dma((iters, 4)), dma((iters, 3)), dma((iters,)),
        dma((HALVES,)), dma((HALVES,)), dma((HALVES, groups)), dma((HALVES, groups)),
        dma((HALVES, chips)), dma((HALVES, chips)),
    ]
    in_vmem = pl.BlockSpec(memory_space=pltpu.VMEM)
    in_smem = pl.BlockSpec(memory_space=pltpu.SMEM)
    anywhere = pl.BlockSpec(memory_space=pltpu.MemorySpace.HBM)
    act, igrad, carried, wgrad = pl.pallas_call(
        functools.partial(kernel, cfg),
        out_shape=(
            jax.ShapeDtypeStruct(features.shape, BF16),
            jax.ShapeDtypeStruct(features.shape, BF16),
            jax.ShapeDtypeStruct((nodes, width), BF16),
            jax.ShapeDtypeStruct((rows if scatter else width, width), F32),
        ),
        in_specs=[in_vmem, in_vmem, in_smem, in_vmem, in_smem, in_vmem, in_smem, anywhere, anywhere],
        out_specs=(in_vmem,) * 4,
        scratch_shapes=scratch,
        compiler_params=pltpu.CompilerParams(
            collective_id=0, has_side_effects=True, vmem_limit_bytes=44 * 1024 * 1024),
        cost_estimate=pl.CostEstimate(flops=6 * 10**9, bytes_accessed=10**7, transcendentals=10**6),
    )(features, adjacency, tile_mask, boundary_adj, boundary_blocks.transpose(0, 2, 3, 1), hub_adj, hub_offsets, weight, cotangent)
    if not scatter:
        wgrad = scale * lax.psum_scatter(wgrad, ("group", "dom"), scatter_dimension=0, tiled=True)
    return act, igrad, carried, wgrad


def solution(mesh):
    return jax.shard_map(
        per_device,
        mesh=mesh,
        in_specs=(
            P(None, ("group", "dom"), None),
            P(("group", "dom"), None),
            P(("group", "dom"), None),
            P(("group", "dom"), None),
            P("group", None, None, None),
            P(None, ("group", "dom")),
            P("group", "dom"),
            P(),
            P(None, ("group", "dom"), None),
        ),
        out_specs=(
            P(None, ("group", "dom"), None),
            P(None, ("group", "dom"), None),
            P(("group", "dom"), None),
            P(("group", "dom"), None),
        ),
        check_vma=False,
    )
```
